256 devices in a mesh: row: 32 (over z, y_hi, core), col: 8 (over x, y_lo).
Axes of the slice: x: 4, y: 4 (y_hi: 2, y_lo: 2; y = y_hi * 2 + y_lo), z: 8, core: 2. Of those that a mesh axis runs over, the one named last changes fastest.
Arguments:
- currents: float32 [8, 131072], P(None, ('row', 'col')), may hold values from -6 to 6
- src_pos: float32 [3, 131072], P(None, ('row', 'col')), may hold values from 0 to 1
- src_dir: float32 [3, 131072], P(None, ('row', 'col')), may hold values from -1 to 1
- cell_ends: int32 [2, 131072], P(None, ('row', 'col')), may hold values from 0 to 65535, as said below
- pan_pos: float32 [3, 65536], P(None, ('row', 'col')), may hold values from 0 to 1
- tgt_pos: float32 [3, 8192], P(None, 'row'), may hold values from 0 to 1
- tgt_dir: float32 [3, 8192], P(None, 'row'), may hold values from -1 to 1
- tgt_ends: int32 [2, 8192], P(None, 'row'), may hold values from 0 to 4095, as said below
- wpan_pos: float32 [3, 4096], P(None, 'row'), may hold values from 0 to 1
Outputs:
- voltage: float32 [8, 8192], P(None, ('row', 'col'))
The draws below stay inside these ranges and needn't reach their ends.
Inputs may be any that keep to these rules, and one draw needn't show every extreme that they name: `cell_ends`: A cell's two panels differ. Source cell j and its panels belong to devices with the same col index: with b = j // 512 and c = p // 256, b and c leave the same remainder on division by 8. `tgt_ends`: A target cell's two panels differ.
All inputs are finite; a program needn't handle non-finite values.
Results may differ from the reference program's by a relative error of at most 0.006.
Values may be sent and summed in bfloat16 or wider, within the bound.
No kernel may reach another device: no remote copies, remote signals or barrier semaphores. Data moves between devices by JAX's collectives and lax.ppermute only.
A program may use at most 64 MiB of HBM per device.

```python
import math
import jax
import jax.numpy as jnp
from jax import lax

CELLS = 131072
PANELS = 65536
PORTS = 4
ROWS = 8192
PROWS = 4096
CELL_DEV = 512
PANEL_DEV = 256
PANEL_BLOCK = 8192


def draw_cell_ends(key, part):
    first_key, step_key = jax.random.split(jax.random.fold_in(key, 11))
    first = jax.random.randint(first_key, (CELLS,), 0, PANEL_BLOCK)
    first = first.at[0].set(0).at[CELLS - 1].set(PANEL_BLOCK - 1)
    offset = jax.random.randint(step_key, (CELLS,), 1, PANEL_BLOCK)
    second = (first + offset) % PANEL_BLOCK
    groups = PANELS // PANEL_BLOCK
    column = jnp.arange(CELLS, dtype=jnp.int32) // CELL_DEV % groups

    def to_global(local):
        return (local // PANEL_DEV * groups + column) * PANEL_DEV + local % PANEL_DEV
    return jnp.stack([to_global(first), to_global(second)]).astype(jnp.int32)


def draw_tgt_ends(key, part):
    first_key, step_key = jax.random.split(jax.random.fold_in(key, 23))
    first = jax.random.randint(first_key, (ROWS,), 0, PROWS)
    first = first.at[0].set(0).at[ROWS - 1].set(PROWS - 1)
    offset = jax.random.randint(step_key, (ROWS,), 1, PROWS)
    second = (first + offset) % PROWS
    return jnp.stack([first, second]).astype(jnp.int32)


def block_scale(own_key, extent, cuts, least, top_value):
    def one(dim, shards_of):
        heights = jax.random.uniform(jax.random.fold_in(jax.random.fold_in(own_key, 6), dim), (shards_of,), jnp.float32, least / len(cuts), top_value / len(cuts))
        return jnp.repeat(jnp.exp(heights), extent[dim] // shards_of).reshape((-1,) + (1,) * (len(extent) - dim - 1))

    level = one(*cuts[0])
    for cut in cuts[1:]:
        level = level * one(*cut)
    return level


def noise(own_key, shape, scale, reach, cuts=(), kind=jnp.bfloat16):
    level = block_scale(own_key, shape, cuts, -0.22, 0.18) if cuts else 1.0
    values = jax.random.normal(own_key, shape, jnp.float32) * scale * level
    return jnp.minimum(jnp.maximum(values, -reach), reach).astype(kind)


def setup_inputs(seed: int = 0) -> dict:
    key_of = jax.random.split(jax.random.key(seed), 10)
    currents = noise(key_of[0], (2 * PORTS, CELLS), 1.0, 6.0, ((1, 256),), jnp.float32)
    src_pos = jnp.clip(1.0 * jax.random.uniform(key_of[1], (3, CELLS), jnp.float32) ** block_scale(key_of[1], (3, CELLS), ((1, 256),), -0.2, 0.2), 0.0, 1.0)
    src_dir = jnp.clip(jax.random.uniform(key_of[2], (3, CELLS), jnp.float32, -1.0, 1.0) * block_scale(key_of[2], (3, CELLS), ((1, 256),), -0.4, 0.0), -1.0, 1.0)
    cell_ends = draw_cell_ends(jax.random.fold_in(key_of[9], 71), 0)
    pan_pos = jnp.clip(1.0 * jax.random.uniform(key_of[4], (3, PANELS), jnp.float32) ** block_scale(key_of[4], (3, PANELS), ((1, 256),), -0.2, 0.2), 0.0, 1.0)
    tgt_pos = jnp.clip(1.0 * jax.random.uniform(key_of[5], (3, ROWS), jnp.float32) ** block_scale(key_of[5], (3, ROWS), ((1, 32),), -0.2, 0.2), 0.0, 1.0)
    tgt_dir = jnp.clip(jax.random.uniform(key_of[6], (3, ROWS), jnp.float32, -1.0, 1.0) * block_scale(key_of[6], (3, ROWS), ((1, 32),), -0.4, 0.0), -1.0, 1.0)
    tgt_ends = draw_tgt_ends(jax.random.fold_in(key_of[9], 71), 0)
    wpan_pos = jnp.clip(1.0 * jax.random.uniform(key_of[8], (3, PROWS), jnp.float32) ** block_scale(key_of[8], (3, PROWS), ((1, 32),), -0.2, 0.2), 0.0, 1.0)
    return dict(currents=currents, src_pos=src_pos, src_dir=src_dir, cell_ends=cell_ends, pan_pos=pan_pos, tgt_pos=tgt_pos, tgt_dir=tgt_dir, tgt_ends=tgt_ends, wpan_pos=wpan_pos)


soft_sq = 0.0004
wave_num = 12.0

def kernel_tile(tpos, spos, tdir, sdir):
    dx = tpos[0][:, None] - spos[0][None, :]
    dy = tpos[1][:, None] - spos[1][None, :]
    dz = tpos[2][:, None] - spos[2][None, :]
    dist_sq = dx * dx + dy * dy + dz * dz + soft_sq
    inverse = lax.rsqrt(dist_sq)
    phase = wave_num * dist_sq * inverse
    real_part = jnp.cos(phase) * inverse
    imag_part = -jnp.sin(phase) * inverse
    if tdir is not None:
        inner = tdir[0][:, None] * sdir[0][None, :] + tdir[1][:, None] * sdir[1][None, :] + tdir[2][:, None] * sdir[2][None, :]
        real_part = real_part * inner
        imag_part = imag_part * inner
    return jnp.concatenate([real_part, imag_part], axis=1).astype(jnp.bfloat16)

def apply_tile(stacked, source):
    half = source.shape[0] // 2
    real_src = source[:half]
    imag_src = source[half:]
    left = jnp.concatenate([jnp.concatenate([real_src, -imag_src], 1), jnp.concatenate([imag_src, real_src], 1)], 0)
    return lax.dot_general(left, stacked, (((1,), (1,)), ((), ())), preferred_element_type=jnp.float32)

def reference(currents, src_pos, src_dir, cell_ends, pan_pos, tgt_pos, tgt_dir, tgt_ends, wpan_pos):
    cur16 = currents.astype(jnp.bfloat16)
    width = min(2048, CELLS)
    count = CELLS // width

    def cell_step(total, index):
        start = (index * width).astype(jnp.int32)
        spos = lax.dynamic_slice_in_dim(src_pos, start, width, 1)
        sdir = lax.dynamic_slice_in_dim(src_dir, start, width, 1)
        source = lax.dynamic_slice_in_dim(cur16, start, width, 1)
        return (total + apply_tile(kernel_tile(tgt_pos, spos, tgt_dir, sdir), source), None)
    induct, _ = lax.scan(cell_step, jnp.zeros((2 * PORTS, ROWS), jnp.float32), jnp.arange(count, dtype=jnp.int32))
    cur_wide = cur16.astype(jnp.float32)
    charges = jnp.zeros((2 * PORTS, PANELS), jnp.float32)
    charges = charges.at[:, cell_ends[0]].add(cur_wide).at[:, cell_ends[1]].add(-cur_wide)
    q16 = charges.astype(jnp.bfloat16)
    pwidth = min(2048, PANELS)
    pcount = PANELS // pwidth

    def panel_step(total, index):
        start = (index * pwidth).astype(jnp.int32)
        ppos = lax.dynamic_slice_in_dim(pan_pos, start, pwidth, 1)
        source = lax.dynamic_slice_in_dim(q16, start, pwidth, 1)
        return (total + apply_tile(kernel_tile(wpan_pos, ppos, None, None), source), None)
    field, _ = lax.scan(panel_step, jnp.zeros((2 * PORTS, PROWS), jnp.float32), jnp.arange(pcount, dtype=jnp.int32))
    pscale = 0.25 / math.sqrt(PANELS)
    lscale = 1.0 / math.sqrt(CELLS)
    potential = jnp.concatenate([field[PORTS:], -field[:PORTS]], 0) * pscale
    voltage = jnp.concatenate([-induct[PORTS:], induct[:PORTS]], 0) * lscale
    return voltage + jnp.take(potential, tgt_ends[0], axis=1) - jnp.take(potential, tgt_ends[1], axis=1)
```

```python
import math

import jax
import jax.numpy as jnp
from jax import lax
from jax.experimental import pallas as pl
from jax.experimental.pallas import tpu as pltpu
from jax.sharding import PartitionSpec as P


CELLS = 131072
PANELS = 65536

SOFT = 0.0004
TURNS = 12.0 / (2.0 * math.pi)
ROOT2 = math.sqrt(2.0)
SIN = tuple(ROOT2 * v for v in (3.141582022121487, -5.167142794774197, 2.5418990103191583, -0.5546361479262166))
COS = tuple(ROOT2 * v for v in (0.999993300552245, -4.9339381816666465, 4.041285139129217, -1.222130017154677))
BF = jnp.bfloat16
F32 = jnp.float32
NT = (((1,), (1,)), ((), ()))
NN = (((1,), (0,)), ((), ()))


def horner(z, coef):
    total = z * coef[-1] + coef[-2]
    for value in coef[-3::-1]:
        total = total * z + value
    return total


def entries(d2):
    inv = lax.rsqrt(d2)
    turns = d2 * inv
    r = turns - jnp.round(turns)
    z = r * r
    s = r * horner(z, SIN)
    c = horner(z, COS)
    t = s * inv
    return (inv - t * s).astype(BF), (t * c).astype(BF)


def split2(x):
    hi = x.astype(BF).astype(F32)
    return hi, (x - hi).astype(BF).astype(F32)


def norm_rows(pos8, extra):
    width = pos8.shape[1]
    whole = pos8[0:3] + pos8[3:6]
    sq = whole * whole
    norm = sq[0:1] + sq[1:2] + sq[2:3] + extra
    m1 = norm.astype(BF).astype(F32)
    rest = norm - m1
    m2 = rest.astype(BF).astype(F32)
    m3 = rest - m2
    row = lax.broadcasted_iota(jnp.int32, (8, width), 0)
    out = jnp.where(row == 0, m1, jnp.where(row == 1, m2, jnp.where(row == 2, m3, 0.0)))
    return jnp.where((row >= 3) & (row < 6), 1.0, out)


def target_features(pos):
    width = pos.shape[1]
    hi, lo = split2((pos - 0.5) * TURNS)
    zero2 = jnp.zeros((2, width), F32)
    norms = norm_rows(jnp.concatenate([hi, lo, zero2], 0), SOFT * TURNS * TURNS)
    swapped = jnp.concatenate([norms[3:6], norms[0:3], zero2], 0)
    rows = jnp.concatenate([-2.0 * hi, -2.0 * hi, zero2, -2.0 * lo, -2.0 * lo, zero2, swapped], 0)
    rows = jnp.concatenate([rows, jnp.zeros((104, width), F32)], 0)
    return rows.T[:, 0:24].astype(BF)


def source_features(pos8):
    return jnp.concatenate([pos8, pos8, norm_rows(pos8, 0.0)], 0).astype(BF)


def turn_ports(re, im):
    half = re.shape[0] // 2
    sign = jnp.where(lax.broadcasted_iota(jnp.int32, re.shape, 0) < half, -1.0, 1.0)
    return im + sign * jnp.concatenate([re[half:], re[:half]], 0)


def side():
    return lax.axis_index("yh")


def pack_kernel(*refs):
    ins, (msg_ref, tgt_ref), bufs, sem = refs[:9], refs[9:11], refs[11:20], refs[20]
    copies = [pltpu.make_async_copy(a, b, sem.at[i]) for i, (a, b) in enumerate(zip(ins, bufs))]
    for copy in copies:
        copy.start()
    for copy in copies:
        copy.wait()
    cur, pos, direction, ends, pan, tpos, tdir, tends, wpos = [ref[...] for ref in bufs]
    hi, lo = split2((pos - 0.5) * TURNS)
    phi, plo = split2((pan - 0.5) * TURNS)
    high = (ends // 2048).astype(F32)
    low = (ends % 256).astype(F32)
    first = jnp.concatenate([hi, lo, high[0:1], low[0:1]], 0)
    second = jnp.concatenate([direction, high[1:2], low[1:2], jnp.concatenate([phi, plo], 1)], 0)
    block = jnp.concatenate([cur, first, second], 0).astype(BF)
    for peer in range(msg_ref.shape[0]):
        msg_ref[peer] = block
    rest = jnp.concatenate([wpos, jnp.zeros((3, 128), F32)], 1)
    tgt_ref[...] = jnp.concatenate([tpos, tdir, tends.astype(F32), rest, jnp.zeros((5, 256), F32)], 0)


def charge_kernel(msg_ref, own_ref, other_ref, acc_ref):
    flip = 2 * side()
    half = lax.broadcasted_iota(jnp.int32, (16, 512), 0) // 8
    lane_id = lax.broadcasted_iota(jnp.int32, (256, 512), 0)
    acc_ref[...] = jnp.zeros_like(acc_ref)

    def gather(step, _):
        left = []
        right = []
        for sub in range(2):
            block = msg_ref[step * 2 + sub].astype(F32)
            cur = block[0:8]
            for end in range(2):
                high = (block[14:15] if end == 0 else block[19:20]).astype(jnp.int32) ^ flip
                low = (block[15:16] if end == 0 else block[20:21]).astype(jnp.int32)
                value = cur if end == 0 else -cur
                two = jnp.concatenate([value, value], 0)
                parts = [jnp.where(half + 2 * j == high, two, 0.0).astype(BF) for j in range(16)]
                left.append(jnp.concatenate(parts, 0))
                right.append(jnp.where(lane_id == low, 1.0, 0.0).astype(BF))
        acc_ref[...] += lax.dot_general(
            jnp.concatenate(left, 1), jnp.concatenate(right, 1), NT, preferred_element_type=F32
        )
        return 0

    lax.fori_loop(0, msg_ref.shape[0] // 2, gather, 0)
    for z in range(8):
        own_ref[z] = acc_ref[z * 32 : z * 32 + 16, :]
        other_ref[z] = acc_ref[z * 32 + 16 : z * 32 + 32, :].astype(BF)


def field_kernel(msg_ref, own_ref, got_ref, tgt_ref, far_ref, out_ref, q_ref):
    blocks = msg_ref.shape[0]
    for z in range(8):
        q_ref[z * 16 : z * 16 + 16, :] = own_ref[z] + got_ref[z].astype(F32)
    wpos = jnp.concatenate([tgt_ref[8:11, 0:128], far_ref[8:11, 0:128]], 1)
    feats = target_features(wpos)
    width = feats.shape[0]
    zero = jnp.zeros((width, 8), F32)

    def sweep(step, carry):
        re, im = carry
        fs = []
        ws = []
        for sub in range(8):
            r = step * 8 + sub
            pan = msg_ref[r].astype(F32)[21:24]
            pos8 = jnp.concatenate([pan[:, :256], pan[:, 256:], jnp.zeros((2, 256), F32)], 0)
            fs.append(source_features(pos8))
            ws.append(q_ref[pl.ds(pl.multiple_of(r * 8, 8), 8), :].astype(BF))
        fs = jnp.concatenate(fs, 1)
        ws = jnp.concatenate(ws, 1)
        d2 = lax.dot_general(feats, fs, NN, preferred_element_type=F32)
        c, s = entries(d2)
        re = re + lax.dot_general(c, ws, NT, preferred_element_type=F32)
        im = im + lax.dot_general(s, ws, NT, preferred_element_type=F32)
        return re, im

    re, im = lax.fori_loop(0, blocks // 8, sweep, (zero, zero))
    both = jnp.concatenate([re, im, jnp.zeros((width, 112), F32)], 1).T
    pot = turn_ports(both[0:8], both[8:16]) * (-0.25 / math.sqrt(PANELS) * TURNS)
    for peer in range(out_ref.shape[0]):
        out_ref[peer] = pot


def induct_kernel(first, count, msg_ref, tgt_ref, far_ref, out_ref, re_ref, im_ref):
    near, far = tgt_ref[...], far_ref[...]
    rows = jnp.concatenate([near, far], 1)
    feats = target_features(rows[0:3])
    re_ref[...] = jnp.zeros_like(re_ref)
    im_ref[...] = jnp.zeros_like(im_ref)
    per = 2

    def sweep(step, _):
        fs = []
        ws = []
        for sub in range(per):
            block = msg_ref[first + step * per + sub].astype(F32)
            fs.append(source_features(block[8:16]))
            cur = block[0:8]
            high = []
            low = []
            for axis in range(3):
                hi, lo = split2(cur * block[16 + axis : 17 + axis])
                high.append(hi)
                low.append(lo)
            ws.append(jnp.concatenate(high + low, 0).astype(BF))
        fs = jnp.concatenate(fs, 1)
        ws = jnp.concatenate(ws, 1)
        d2 = lax.dot_general(feats, fs, NN, preferred_element_type=F32)
        c, s = entries(d2)
        re_ref[...] += lax.dot_general(c, ws, NT, preferred_element_type=F32)
        im_ref[...] += lax.dot_general(s, ws, NT, preferred_element_type=F32)
        return 0

    lax.fori_loop(0, count // per, sweep, 0)
    pad = jnp.zeros((feats.shape[0], 80), F32)
    re = jnp.concatenate([re_ref[...], pad], 1).T
    im = jnp.concatenate([im_ref[...], pad], 1).T
    re = re[0:24] + re[24:48]
    im = im[0:24] + im[24:48]
    tdir = rows[3:6]
    re = tdir[0:1] * re[0:8] + tdir[1:2] * re[8:16] + tdir[2:3] * re[16:24]
    im = tdir[0:1] * im[0:8] + tdir[1:2] * im[8:16] + tdir[2:3] * im[16:24]
    out_ref[...] = turn_ports(re, im) * (TURNS / math.sqrt(CELLS))


def join_kernel(ind_ref, more_ref, pot_ref, tgt_ref, far_ref, out_ref):
    blocks = pot_ref.shape[0]
    yh = side()
    ends = jnp.concatenate([tgt_ref[6:8], far_ref[6:8]], 1).astype(jnp.int32)
    width = ends.shape[1]
    volt = ind_ref[...] + more_ref[...]
    row_id = lax.broadcasted_iota(jnp.int32, (128, width), 0)
    high = ends // 128
    low = ends % 128
    left = []
    for i in range(blocks):
        pair = pot_ref[i]
        for j in range(2):
            hi, lo = split2(pair[:, j * 128 : j * 128 + 128])
            left += [hi, lo]
    left = jnp.concatenate(left, 0).astype(BF)
    for end in range(2):
        pick = jnp.where(row_id == low[end : end + 1], 1.0, 0.0).astype(BF)
        found = lax.dot_general(left, pick, NN, preferred_element_type=F32)
        total = jnp.zeros((16, width), F32)
        for i in range(blocks):
            for j in range(2):
                panel = (i // 2) * 4 + (yh ^ j) * 2 + i % 2
                at = (i * 2 + j) * 16
                total = total + jnp.where(high[end : end + 1] == panel, found[at : at + 16], 0.0)
        both = total[0:8] + total[8:16]
        volt = volt + both if end == 0 else volt - both
    blank = jnp.zeros((8, 96), F32)
    for j in range(2):
        for col in range(8):
            at = j * 256 + col * 32
            out_ref[(yh ^ j) * 8 + col] = jnp.concatenate([volt[:, at : at + 32], blank], 1)


def total_kernel(parts_ref, out_ref):
    total = parts_ref[0]
    for peer in range(1, parts_ref.shape[0]):
        total = total + parts_ref[peer]
    out_ref[...] = total[:, : out_ref.shape[1]]


def call(kernel, outs, scratch=(), **extra):
    return pl.pallas_call(
        kernel,
        out_shape=tuple(jax.ShapeDtypeStruct(shape, dtype) for shape, dtype in outs),
        scratch_shapes=scratch,
        compiler_params=pltpu.CompilerParams(vmem_limit_bytes=48 << 20),
        **extra,
    )


def plan(*args):
    near = ("z", "core")
    last = ("yh", "x", "yl")
    swap = [(0, 1), (1, 0)]
    hbm = pl.BlockSpec(memory_space=pltpu.HBM)
    msg, tgt = call(
        pack_kernel, [((16, 24, 512), BF), ((16, 256), F32)],
        tuple(pltpu.VMEM(a.shape, a.dtype) for a in args) + (pltpu.SemaphoreType.DMA((9,)),),
        in_specs=[hbm] * 9,
    )(*[pltpu.with_memory_space_constraint(a, pltpu.HBM) for a in args])
    far = lax.ppermute(tgt, "yh", swap)
    msg = lax.all_to_all(msg, near, 0, 0, tiled=True)
    own, other = call(
        charge_kernel, [((8, 16, 256), F32), ((8, 16, 256), BF)], (pltpu.VMEM((256, 256), F32),)
    )(msg)
    got = lax.ppermute(other, "yh", swap)

    def induct(first, count):
        acc = pltpu.VMEM((512, 48), F32)
        kernel = lambda *refs: induct_kernel(first, count, *refs)
        return call(kernel, [((8, 512), F32)], (acc, acc))(msg, tgt, far)[0]

    ind = induct(0, 4)
    pot, = call(field_kernel, [((16, 8, 256), F32)], (pltpu.VMEM((128, 256), F32),))(
        msg, own, got, tgt, far
    )
    pot = lax.all_to_all(pot, near, 0, 0, tiled=True)
    more = induct(4, 12)
    parts, = call(join_kernel, [((16, 8, 128), F32)])(ind, more, pot, tgt, far)
    parts = lax.all_to_all(parts, last, 0, 0, tiled=True)
    return call(total_kernel, [((8, 32), F32)])(parts)[0]


def solution(mesh):
    names = ("z", "yh", "core", "x", "yl")
    fine = jax.sharding.Mesh(mesh.devices.reshape(8, 2, 2, 4, 2), names)
    both = P(None, names)
    row = P(None, names[:3])
    return jax.shard_map(
        plan,
        mesh=fine,
        in_specs=(both, both, both, both, both, row, row, row, row),
        out_specs=both,
        check_vma=False,
    )
```
